32 devices in a mesh: groups: 2 (over y), blk: 4 (over z), head: 4 (over x, core).
Axes of the slice: x: 2, y: 2, z: 4, core: 2. Of those that a mesh axis runs over, the one named last changes fastest.
Arguments:
- queries: bfloat16 [4096, 4096], P(('groups', 'blk', 'head')), parts along dimension 0, may hold values from -8 to 8
- keys: bfloat16 [4096, 4096], P(('groups', 'blk', 'head')), parts along dimension 0, may hold values from -8 to 8
- values: bfloat16 [4096, 4096], P(('groups', 'blk', 'head')), parts along dimension 0, may hold values from -6 to 6
- scale_qk: float32 [4096], replicated, may hold values from 0.7 to 8
- w_out: bfloat16 [4096, 4096], P('head'), may hold values from -0.09375 to 0.09375
- stretch_start: int32 [32], P(('groups', 'blk', 'head')), parts along dimension 0, may hold values from 0 to 1920, as said below
Outputs:
- attended: bfloat16 [4096, 4096], P(('groups', 'blk', 'head')), parts along dimension 0
The draws below stay inside these ranges and needn't reach their ends.
There are 2 independent parts, one for each index of `groups`. The reference program is written for one: setup_inputs(seed, part) draws one part's arguments, and reference() takes and returns one part's arrays. A program takes and returns all parts, laid end to end along the dimension named above; an argument that names none is the same for every part. Nothing has to cross between parts.
Inputs may be any that keep to these rules, and one draw needn't show every extreme that they name: stretch_start[b * 4 + h] = (((b + r) % 4) * 4 + h) * 128 for an offset r of 0 to 3 drawn from the seed.
All inputs are finite; a program needn't handle non-finite values.
Results may differ from the reference program's by a relative error of at most 0.04.
Values may be sent and summed in bfloat16 or wider, within the bound.
A program may use at most 128 MiB of HBM per device.

```python
import jax
import jax.numpy as jnp
from jax import lax

D = 4096
H = 32
DH = 128
TOK_DEV = 128
SEGMENTS = 4
HEAD_GROUPS = 4
SEG = 512
WIN = 1024
SEQ = 2048
HL = 8


def paired(key):
    base_q = jax.random.normal(jax.random.fold_in(key, 11), (SEQ, H * DH), jnp.float32)
    base_k = jax.random.normal(jax.random.fold_in(key, 12), (SEQ, H * DH), jnp.float32)
    return (jnp.clip(base_q, -8.0, 8.0), jnp.clip(base_k, -8.0, 8.0))


def draw_queries(key, part):
    return paired(key)[0].astype(jnp.bfloat16)


def draw_keys(key, part):
    return paired(key)[1].astype(jnp.bfloat16)


def draw_scale_qk(key, part):
    return jax.random.uniform(key, (H * DH,), jnp.float32, 0.7, 1.4)


def draw_stretch_start(key, part):
    halves = jax.random.randint(jax.random.fold_in(key, 21), (), 0, SEGMENTS // 2).astype(jnp.int32)
    offset = (halves * 2 + jnp.asarray(part, jnp.int32) % 2).astype(jnp.int32)
    order = (jnp.arange(SEGMENTS, dtype=jnp.int32) + offset) % SEGMENTS
    inner = jnp.arange(HEAD_GROUPS, dtype=jnp.int32)
    starts = (order[:, None] * HEAD_GROUPS + inner[None, :]) * TOK_DEV
    return starts.reshape(-1).astype(jnp.int32)


def steps_of(own_key, shape, cuts, low, top_value):
    def one(position, shards_of):
        draws = jax.random.uniform(jax.random.fold_in(jax.random.fold_in(own_key, 6), position), (shards_of,), jnp.float32, low / len(cuts), top_value / len(cuts))
        return jnp.repeat(jnp.exp(draws), shape[position] // shards_of).reshape((-1,) + (1,) * (len(shape) - position - 1))

    gain = one(*cuts[0])
    for cut in cuts[1:]:
        gain = gain * one(*cut)
    return gain


def bell_draw(key, dims, scale, bound, split=(), kind=jnp.bfloat16):
    loudness = steps_of(key, dims, split, -0.22, 0.18) if split else 1.0
    result = jax.random.normal(key, dims, jnp.float32) * scale * loudness
    return jnp.minimum(jnp.maximum(result, -bound), bound).astype(kind)


def setup_inputs(seed: int = 0, part: int = 0) -> dict:
    key_of = jax.random.split(jax.random.key(seed), 7)
    part_splits = jax.random.split(jax.random.fold_in(key_of[6], part), 7)
    return {
        "queries": draw_queries(jax.random.fold_in(jax.random.fold_in(key_of[6], part), 71), part),
        "keys": draw_keys(jax.random.fold_in(jax.random.fold_in(key_of[6], part), 71), part),
        "values": bell_draw(part_splits[2], (SEQ, H * DH), 1.0, 6.0, ((0, 16),)),
        "scale_qk": draw_scale_qk(jax.random.fold_in(key_of[6], 71), part),
        "w_out": bell_draw(key_of[4], (H * DH, D), (H * DH) ** -0.5, 0.09375, ((0, 4),)),
        "stretch_start": draw_stretch_start(jax.random.fold_in(jax.random.fold_in(key_of[6], part), 71), part),
    }


def normalize(rows, scale_qk):
    x = rows.astype(jnp.float32).reshape(rows.shape[0], H, DH)
    x = x * lax.rsqrt(lax.optimization_barrier(jnp.mean(x * x, axis=2, keepdims=True)) + 1e-06)
    return (x.reshape(rows.shape[0], H * DH) * scale_qk[None, :]).astype(jnp.bfloat16)

def reference(queries, keys, values, scale_qk, w_out, stretch_start):
    qn = normalize(queries, scale_qk)
    kn = normalize(keys, scale_qk)
    offsets = jnp.arange(TOK_DEV, dtype=jnp.int32)
    pos = (stretch_start[:, None] + offsets[None, :]).reshape(-1).astype(jnp.int32)
    order = jnp.argsort(pos).astype(jnp.int32)
    q_sorted = qn[order]
    k_sorted = jnp.concatenate([jnp.zeros((WIN, H * DH), jnp.bfloat16), kn[order]], axis=0)
    v_sorted = jnp.concatenate([jnp.zeros((WIN, H * DH), jnp.bfloat16), values[order]], axis=0)
    sorted_pos = pos[order]
    padded_pos = jnp.concatenate([jnp.full((WIN,), -3 * WIN, jnp.int32), sorted_pos], axis=0)
    blocks = SEQ // SEG
    inverse = 1.0 / DH ** 0.5

    def block_out(index):
        head = index // blocks
        block = index % blocks
        first_col = (head * DH).astype(jnp.int32)
        first_row = (block * SEG).astype(jnp.int32)
        q_head = lax.dynamic_slice(q_sorted, (first_row, first_col), (SEG, DH))
        k_head = lax.dynamic_slice(k_sorted, (first_row, first_col), (WIN + SEG, DH))
        v_head = lax.dynamic_slice(v_sorted, (first_row, first_col), (WIN + SEG, DH))
        q_pos = lax.dynamic_slice_in_dim(sorted_pos, first_row, SEG, 0)
        k_pos = lax.dynamic_slice_in_dim(padded_pos, first_row, WIN + SEG, 0)
        allowed = (k_pos[None, :] <= q_pos[:, None]) & (q_pos[:, None] - k_pos[None, :] < WIN)
        scores = jnp.dot(q_head, k_head.T, preferred_element_type=jnp.float32) * inverse
        peak = lax.optimization_barrier(jnp.max(jnp.where(allowed, scores, -1e+30), axis=1, keepdims=True))
        weights = jnp.where(allowed, jnp.exp(scores - peak), jnp.float32(0.0))
        total = lax.optimization_barrier(jnp.sum(weights, axis=1, keepdims=True))
        mixed = jnp.dot(weights.astype(jnp.bfloat16), v_head, preferred_element_type=jnp.float32)
        return (mixed / total).astype(jnp.bfloat16)
    stacked = lax.map(block_out, jnp.arange(H * blocks, dtype=jnp.int32))
    stacked = stacked.reshape(H, SEQ, DH)
    sorted_out = jnp.transpose(stacked, (1, 0, 2)).reshape(SEQ, H * DH)
    heads_out = sorted_out[pos]
    width = HL * DH
    summed = jnp.zeros((SEQ, D), jnp.float32)
    for group in range(HEAD_GROUPS):
        part = jnp.dot(heads_out[:, group * width:(group + 1) * width], w_out[group * width:(group + 1) * width, :], preferred_element_type=jnp.float32)
        part = lax.optimization_barrier(part.astype(jnp.bfloat16))
        summed = summed + part.astype(jnp.float32)
    return summed.astype(jnp.bfloat16)
```

```python
import functools

import jax
import jax.numpy as jnp
from jax import lax
from jax.experimental import pallas as pl
from jax.experimental.pallas import tpu as pltpu
from jax.sharding import PartitionSpec as P

DH = 128
SCORE = 1.4426950408889634 / DH**0.5
NC = 2


def kernel(
    nh, nb, q_hbm, k_hbm, v_hbm, scale_ref, w_hbm, start_ref, out_ref,
    qin, kin, qn, kn, w_ref, qseg, kbuf, vbuf, ho, sib_out, sib_in, comb, rbuf,
    load_sem, loc_sem, a2a_s, a2a_r, h1_s, h1_r, h2_s, h2_r, sib_s, sib_r, red_s, red_r,
):
    t, hd = qin.shape
    cols = hd // nh
    heads = cols // DH
    seg = nh * t
    win = 2 * seg + t
    width = w_ref.shape[1]
    half = width // 2
    chunk = half // NC
    nx = nh // 2
    me = lax.axis_index("head")
    z = lax.axis_index("blk")
    chip = me // 2
    core = me % 2
    sib = chip * 2 + (1 - core)
    nxt = (z + 1) % nb
    prv = (z + nb - 1) % nb

    def partner(jx, jc):
        return ((chip + jx) % nx) * 2 + (core + jc) % 2

    others = [(jx, 0) for jx in range(1, nx)] + [(jx, 1) for jx in range(nx)]
    arrival = [(jx, jc) for jx in range(nx) for jc in range(2) if jx or jc]

    loads = [
        pltpu.make_async_copy(k_hbm, kin, load_sem.at[0]),
        pltpu.make_async_copy(q_hbm, qin, load_sem.at[1]),
        pltpu.make_async_copy(w_hbm, w_ref, load_sem.at[2]),
    ]
    for copy in loads:
        copy.start()

    barrier = pltpu.get_barrier_semaphore()
    for jx, jc in others:
        pl.semaphore_signal(barrier, inc=1, device_id={"head": partner(jx, jc)})
    pl.semaphore_signal(barrier, inc=1, device_id={"blk": nxt})
    pl.semaphore_signal(barrier, inc=1, device_id={"blk": prv})
    pl.semaphore_wait(barrier, nh + 1)

    def group(ref, peer):
        return ref.at[:, pl.ds(pl.multiple_of(peer * cols, DH), cols)]

    def piece(ref, base, index):
        return ref.at[pl.ds(pl.multiple_of(base + index * t, t), t), :]

    def swap(kind, src, dst, base, peer, source):
        return pltpu.make_async_remote_copy(
            src_ref=group(src, peer), dst_ref=piece(dst, base, source),
            send_sem=a2a_s.at[kind, peer], recv_sem=a2a_r.at[kind, source],
            device_id={"head": peer},
        )

    def hop(src, dst, kind, base, index, send, recv):
        return pltpu.make_async_remote_copy(
            src_ref=src, dst_ref=piece(dst, base, index),
            send_sem=send.at[kind, index], recv_sem=recv.at[kind, index],
            device_id={"blk": nxt},
        )

    def normed(src, dst, peer):
        for h in range(heads):
            at = pl.ds(pl.multiple_of(peer * cols + h * DH, DH), DH)
            x = src[:, at].astype(jnp.float32)
            x = x * lax.rsqrt(jnp.mean(x * x, axis=1, keepdims=True) + 1e-06)
            dst[:, at] = (x * scale_ref[:, at]).astype(jnp.bfloat16)

    hop(group(v_hbm, me), vbuf, 1, seg, me, h1_s, h1_r).start()
    for jx, jc in others:
        swap(1, v_hbm, vbuf, 2 * seg, partner(jx, jc), me).start()
    own_v = pltpu.make_async_copy(group(v_hbm, me), piece(vbuf, 2 * seg, me), loc_sem.at[1])
    own_v.start()

    loads[0].wait()
    normed(kin, kn, me)
    hop(group(kn, me), kbuf, 0, seg, me, h1_s, h1_r).start()
    own_k = pltpu.make_async_copy(group(kn, me), piece(kbuf, 2 * seg, me), loc_sem.at[0])
    own_k.start()
    for jx, jc in others:
        peer = partner(jx, jc)
        normed(kin, kn, peer)
        swap(0, kn, kbuf, 2 * seg, peer, me).start()

    loads[1].wait()
    for jx, jc in others:
        peer = partner(jx, jc)
        normed(qin, qn, peer)
        swap(2, qn, qseg, 0, peer, me).start()
    normed(qin, qn, me)
    own_q = pltpu.make_async_copy(group(qn, me), piece(qseg, 0, me), loc_sem.at[2])
    own_q.start()

    for jx, jc in arrival:
        source = partner(jx, jc)
        swap(1, v_hbm, vbuf, 2 * seg, source, source).wait_recv()
        hop(piece(vbuf, 2 * seg, source), vbuf, 1, seg, source, h1_s, h1_r).start()
        swap(0, kn, kbuf, 2 * seg, source, source).wait_recv()
        hop(piece(kbuf, 2 * seg, source), kbuf, 0, seg, source, h1_s, h1_r).start()

    def relay(step, carry):
        i = nh - 1 - step
        for kind, buf in ((0, kbuf), (1, vbuf)):
            hop(piece(buf, 2 * seg, i), buf, kind, seg, i, h1_s, h1_r).wait_recv()
            hop(piece(buf, seg, i), buf, kind, 0, i, h2_s, h2_r).start()
        return carry

    lax.fori_loop(0, nh, relay, 0)
    for jx, jc in arrival:
        source = partner(jx, jc)
        swap(2, qn, qseg, 0, source, source).wait_recv()
    own_q.wait()
    own_k.wait()
    own_v.wait()
    loads[2].wait()

    first = start_ref[0] - me * t
    row = lax.broadcasted_iota(jnp.int32, (t, win), 0)
    col = lax.broadcasted_iota(jnp.int32, (t, win), 1)

    def to_sibling(i, c):
        at = pl.ds(c * chunk, chunk)
        return pltpu.make_async_remote_copy(
            src_ref=sib_out.at[i, :, at], dst_ref=sib_in.at[i, :, at],
            send_sem=sib_s.at[i, c], recv_sem=sib_r.at[i, c],
            device_id={"head": sib},
        )

    def to_owner(i, c, source, owner):
        at = pl.ds(c * chunk, chunk)
        return pltpu.make_async_remote_copy(
            src_ref=comb.at[i, :, at], dst_ref=rbuf.at[source, :, at],
            send_sem=red_s.at[i, c], recv_sem=red_r.at[source, c],
            device_id={"head": owner},
        )

    def block(step, carry):
        i = nh - 1 - step
        for kind, buf in ((0, kbuf), (1, vbuf)):
            hop(piece(buf, seg, i), buf, kind, 0, i, h2_s, h2_r).wait_recv()
        rows = pl.ds(pl.multiple_of(i * t, t), t)
        keys = pl.ds(pl.multiple_of(i * t, t), win)
        allowed = (col > row) & (col <= row + 2 * seg) & (col >= 2 * seg - first - i * t)
        for h in range(heads):
            at = pl.ds(h * DH, DH)
            s = lax.dot_general(
                qseg[rows, at], kbuf[keys, at], (((1,), (1,)), ((), ())),
                preferred_element_type=jnp.float32,
            )
            s = jnp.where(allowed, s, -1e30)
            p = jnp.exp2((s - jnp.max(s, axis=1, keepdims=True)) * SCORE)
            total = jnp.sum(p, axis=1, keepdims=True)
            o = jnp.dot(p.astype(jnp.bfloat16), vbuf[keys, at], preferred_element_type=jnp.float32)
            ho[:, at] = (o / total).astype(jnp.bfloat16)

        def project(side, c):
            at = pl.ds(pl.multiple_of(side * half + c * chunk, DH), chunk)
            return jnp.dot(ho[...], w_ref[:, at], preferred_element_type=jnp.float32)

        for c in range(NC):
            sib_out[i, :, pl.ds(c * chunk, chunk)] = project(1 - core, c).astype(jnp.bfloat16)
            to_sibling(i, c).start()
        for c in range(NC):
            at = pl.ds(c * chunk, chunk)
            mine = project(core, c)
            to_sibling(i, c).wait_recv()
            both = (mine + sib_in[i, :, at].astype(jnp.float32)).astype(jnp.bfloat16)

            @pl.when(me == i)
            def _():
                rbuf[me, :, at] = both

            @pl.when(me != i)
            def _():
                comb[i, :, at] = both
                to_owner(i, c, me, i).start()

        return carry

    lax.fori_loop(0, nh, block, 0)

    for c in range(NC):
        at = pl.ds(c * chunk, chunk)
        for jx, jc in arrival:
            source = partner(jx, jc)
            to_owner(source, c, source, source).wait_recv()
        for side in range(2):
            total = rbuf[side, :, at].astype(jnp.float32)
            for x in range(1, nx):
                total = total + rbuf[2 * x + side, :, at].astype(jnp.float32)
            out_ref[:, pl.ds(side * half + c * chunk, chunk)] = total.astype(jnp.bfloat16)

    for jx, jc in arrival:
        peer = partner(jx, jc)
        swap(1, v_hbm, vbuf, 2 * seg, peer, me).wait_send()
        swap(0, kn, kbuf, 2 * seg, peer, me).wait_send()
        swap(2, qn, qseg, 0, peer, me).wait_send()
        for c in range(NC):
            to_owner(peer, c, me, peer).wait_send()

    def sent(i, carry):
        for kind, buf in ((0, kbuf), (1, vbuf)):
            hop(piece(buf, 2 * seg, i), buf, kind, seg, i, h1_s, h1_r).wait_send()
            hop(piece(buf, seg, i), buf, kind, 0, i, h2_s, h2_r).wait_send()
        for c in range(NC):
            to_sibling(i, c).wait_send()
        return carry

    lax.fori_loop(0, nh, sent, 0)


def solution(mesh):
    nh = mesh.shape["head"]
    nb = mesh.shape["blk"]

    def shards(queries, keys, values, scale_qk, w_out, stretch_start):
        t, hd = queries.shape
        cols = hd // nh
        seg = nh * t
        width = w_out.shape[1]
        half = width // 2
        bf16 = jnp.bfloat16
        dma = pltpu.SemaphoreType.DMA
        anywhere = pl.BlockSpec(memory_space=pl.ANY)
        vmem = pl.BlockSpec(memory_space=pltpu.VMEM)
        return pl.pallas_call(
            functools.partial(kernel, nh, nb),
            out_shape=jax.ShapeDtypeStruct((t, width), bf16),
            in_specs=[anywhere, anywhere, anywhere, vmem, anywhere,
                      pl.BlockSpec(memory_space=pltpu.SMEM)],
            out_specs=vmem,
            scratch_shapes=[
                pltpu.VMEM((t, hd), bf16),
                pltpu.VMEM((t, hd), bf16),
                pltpu.VMEM((t, hd), bf16),
                pltpu.VMEM((t, hd), bf16),
                pltpu.VMEM((cols, width), bf16),
                pltpu.VMEM((seg, cols), bf16),
                pltpu.VMEM((3 * seg, cols), bf16),
                pltpu.VMEM((3 * seg, cols), bf16),
                pltpu.VMEM((t, cols), bf16),
                pltpu.VMEM((nh, t, half), bf16),
                pltpu.VMEM((nh, t, half), bf16),
                pltpu.VMEM((nh, t, half), bf16),
                pltpu.VMEM((nh, t, half), bf16),
                dma((3,)),
                dma((3,)),
                dma((3, nh)),
                dma((3, nh)),
                dma((2, nh)),
                dma((2, nh)),
                dma((2, nh)),
                dma((2, nh)),
                dma((nh, NC)),
                dma((nh, NC)),
                dma((nh, NC)),
                dma((nh, NC)),
            ],
            compiler_params=pltpu.CompilerParams(
                collective_id=0, has_side_effects=True, vmem_limit_bytes=56 * 1024 * 1024
            ),
        )(queries, keys, values, scale_qk.reshape(1, hd), w_out, stretch_start)

    return jax.shard_map(
        shards,
        mesh=mesh,
        in_specs=(
            P(("groups", "blk", "head"), None),
            P(("groups", "blk", "head"), None),
            P(("groups", "blk", "head"), None),
            P(),
            P("head", None),
            P(("groups", "blk", "head")),
        ),
        out_specs=P(("groups", "blk", "head"), None),
        check_vma=False,
    )
```

```python
import functools

import jax
import jax.numpy as jnp
from jax import lax
from jax.experimental import pallas as pl
from jax.experimental.pallas import tpu as pltpu
from jax.sharding import PartitionSpec as P

DH = 128
SCORE = 1.4426950408889634 / DH**0.5
NC = 2
NS = 2


def kernel(
    nh, nb, q_hbm, k_hbm, v_hbm, scale_ref, w_hbm, start_ref, rbuf,
    qin, kin, qn, kn, w_ref, qseg, kbuf, vbuf, acc, ho, sib_out, sib_in, comb,
    load_sem, loc_sem, keep_sem, a2a_s, a2a_r, h1_s, h1_r, h2_s, h2_r, sib_s, sib_r, red_s, red_r,
):
    t, hd = qin.shape
    cols = hd // nh
    heads = cols // DH
    seg = nh * t
    sub = t // NS
    width = w_ref.shape[1]
    half = width // 2
    chunk = half // NC
    nx = nh // 2
    me = lax.axis_index("head")
    z = lax.axis_index("blk")
    chip = me // 2
    core = me % 2
    sib = chip * 2 + (1 - core)
    nxt = (z + 1) % nb
    prv = (z + nb - 1) % nb

    def partner(jx, jc):
        return ((chip + jx) % nx) * 2 + (core + jc) % 2

    others = [(jx, 0) for jx in range(1, nx)] + [(jx, 1) for jx in range(nx)]
    arrival = [(jx, jc) for jx in range(nx) for jc in range(2) if jx or jc]

    loads = [
        pltpu.make_async_copy(k_hbm, kin, load_sem.at[0]),
        pltpu.make_async_copy(q_hbm, qin, load_sem.at[1]),
        pltpu.make_async_copy(w_hbm, w_ref, load_sem.at[2]),
    ]
    for copy in loads:
        copy.start()

    barrier = pltpu.get_barrier_semaphore()
    for jx, jc in others:
        pl.semaphore_signal(barrier, inc=1, device_id={"head": partner(jx, jc)})
    pl.semaphore_signal(barrier, inc=1, device_id={"blk": nxt})
    pl.semaphore_signal(barrier, inc=1, device_id={"blk": prv})
    pl.semaphore_wait(barrier, nh + 1)

    def group(ref, peer):
        return ref.at[:, pl.ds(pl.multiple_of(peer * cols, DH), cols)]

    def piece(ref, base, index):
        return ref.at[pl.ds(pl.multiple_of(base + index * t, t), t), :]

    def swap(kind, src, dst, base, peer, source):
        return pltpu.make_async_remote_copy(
            src_ref=group(src, peer), dst_ref=piece(dst, base, source),
            send_sem=a2a_s.at[kind, peer], recv_sem=a2a_r.at[kind, source],
            device_id={"head": peer},
        )

    def hop(src, dst, kind, base, index, send, recv):
        return pltpu.make_async_remote_copy(
            src_ref=src, dst_ref=piece(dst, base, index),
            send_sem=send.at[kind, index], recv_sem=recv.at[kind, index],
            device_id={"blk": nxt},
        )

    def normed(src, dst, peer):
        for h in range(heads):
            at = pl.ds(pl.multiple_of(peer * cols + h * DH, DH), DH)
            x = src[:, at].astype(jnp.float32)
            x = x * lax.rsqrt(jnp.mean(x * x, axis=1, keepdims=True) + 1e-06)
            dst[:, at] = (x * scale_ref[:, at]).astype(jnp.bfloat16)

    hop(group(v_hbm, me), vbuf, 1, seg, me, h1_s, h1_r).start()
    for jx, jc in others:
        swap(1, v_hbm, vbuf, 2 * seg, partner(jx, jc), me).start()
    own_v = pltpu.make_async_copy(group(v_hbm, me), piece(vbuf, 2 * seg, me), loc_sem.at[1])
    own_v.start()

    loads[0].wait()
    normed(kin, kn, me)
    hop(group(kn, me), kbuf, 0, seg, me, h1_s, h1_r).start()
    own_k = pltpu.make_async_copy(group(kn, me), piece(kbuf, 2 * seg, me), loc_sem.at[0])
    own_k.start()
    for jx, jc in others:
        peer = partner(jx, jc)
        normed(kin, kn, peer)
        swap(0, kn, kbuf, 2 * seg, peer, me).start()

    loads[1].wait()
    for jx, jc in [(0, 0)] + others:
        normed(qin, qn, partner(jx, jc))
    own_q = pltpu.make_async_copy(group(qn, me), piece(qseg, 0, me), loc_sem.at[2])
    own_q.start()

    def onward(kind, src, buf, jx, jc):
        source = partner(jx, jc)
        swap(kind, src, buf, 2 * seg, source, source).wait_recv()
        hop(piece(buf, 2 * seg, source), buf, kind, seg, source, h1_s, h1_r).start()

    onward(1, v_hbm, vbuf, 0, 1)
    onward(0, kn, kbuf, 0, 1)
    for jx, jc in arrival[1:]:
        onward(1, v_hbm, vbuf, jx, jc)
    for jx, jc in arrival[1:]:
        onward(0, kn, kbuf, jx, jc)
    for jx, jc in others:
        peer = partner(jx, jc)
        swap(2, qn, qseg, 0, peer, me).start()

    def slab(ref, base, i, part):
        return ref.at[pl.ds(pl.multiple_of(base + i * t + part * sub, sub), sub), :]

    def pass_on(kind, buf, i, part):
        return pltpu.make_async_remote_copy(
            src_ref=slab(buf, seg, i, part), dst_ref=slab(buf, 0, i, part),
            send_sem=h2_s.at[kind, i, part], recv_sem=h2_r.at[kind, i, part],
            device_id={"blk": nxt},
        )

    def relay(step, carry):
        i = nh - 1 - step
        for kind, buf in ((0, kbuf), (1, vbuf)):
            hop(piece(buf, 2 * seg, i), buf, kind, seg, i, h1_s, h1_r).wait_recv()
        for part in reversed(range(NS)):
            for kind, buf in ((0, kbuf), (1, vbuf)):
                pass_on(kind, buf, i, part).start()
        return carry

    lax.fori_loop(0, nh, relay, 0)
    for jx, jc in arrival:
        source = partner(jx, jc)
        swap(2, qn, qseg, 0, source, source).wait_recv()
    own_q.wait()
    own_k.wait()
    own_v.wait()
    loads[2].wait()

    first = start_ref[0] - me * t
    row = lax.broadcasted_iota(jnp.int32, (t, 2 * seg), 0)
    col = lax.broadcasted_iota(jnp.int32, (t, 2 * seg), 1)

    def to_sibling(i, part, c):
        at = (i, pl.ds(part * sub, sub), pl.ds(c * chunk, chunk))
        return pltpu.make_async_remote_copy(
            src_ref=sib_out.at[at], dst_ref=sib_in.at[at],
            send_sem=sib_s.at[i, part, c], recv_sem=sib_r.at[i, part, c],
            device_id={"head": sib},
        )

    def home(x, side, part, c):
        columns = pl.ds(pl.multiple_of(side * half + c * chunk, DH), chunk)
        return rbuf.at[x, pl.ds(part * sub, sub), columns]

    def to_owner(i, part, c, source, owner):
        return pltpu.make_async_remote_copy(
            src_ref=comb.at[i, pl.ds(part * sub, sub), pl.ds(c * chunk, chunk)],
            dst_ref=home(source // 2, source % 2, part, c),
            send_sem=red_s.at[i, part, c], recv_sem=red_r.at[source, part, c],
            device_id={"head": owner},
        )

    def keep(i, part, c):
        return pltpu.make_async_copy(
            comb.at[i, pl.ds(part * sub, sub), pl.ds(c * chunk, chunk)],
            home(chip, core, part, c), keep_sem.at[part, c],
        )

    def block(step, carry):
        i = nh - 1 - step
        rows = pl.ds(pl.multiple_of(i * t, t), t)
        keys = pl.ds(pl.multiple_of(i * t + t, t), 2 * seg)
        oldest = 2 * seg - first - i * t
        allowed = (col <= row + (2 * seg - t)) & (col >= oldest - t)
        held = []
        for h in range(heads):
            at = pl.ds(h * DH, DH)
            s = lax.dot_general(
                qseg[rows, at], kbuf[keys, at], (((1,), (1,)), ((), ())),
                preferred_element_type=jnp.float32,
            )
            s = jnp.where(allowed, s, -1e30)
            peak = jnp.max(s, axis=1, keepdims=True)
            p = jnp.exp2((s - peak) * SCORE)
            held.append((peak, jnp.sum(p, axis=1, keepdims=True)))
            acc[:, at] = jnp.dot(
                p.astype(jnp.bfloat16), vbuf[keys, at], preferred_element_type=jnp.float32
            )

        for part in reversed(range(NS)):
            for kind, buf in ((0, kbuf), (1, vbuf)):
                pass_on(kind, buf, i, part).wait_recv()
            low = part * sub
            many = t - low
            keys = pl.ds(pl.multiple_of(i * t + low, sub), many)
            here = pl.ds(pl.multiple_of(i * t + low, sub), sub)
            age = lax.broadcasted_iota(jnp.int32, (sub, many), 1)
            allowed = (age > lax.broadcasted_iota(jnp.int32, (sub, many), 0)) & (
                age >= oldest - low
            )
            for h in range(heads):
                at = pl.ds(h * DH, DH)
                s = lax.dot_general(
                    qseg[here, at], kbuf[keys, at], (((1,), (1,)), ((), ())),
                    preferred_element_type=jnp.float32,
                )
                s = jnp.where(allowed, s, -1e30)
                peak, total = (value[low:low + sub] for value in held[h])
                top = jnp.maximum(peak, jnp.max(s, axis=1, keepdims=True))
                p = jnp.exp2((s - top) * SCORE)
                fade = jnp.exp2((peak - top) * SCORE)
                total = total * fade + jnp.sum(p, axis=1, keepdims=True)
                o = acc[pl.ds(low, sub), at] * fade + jnp.dot(
                    p.astype(jnp.bfloat16), vbuf[keys, at], preferred_element_type=jnp.float32
                )
                ho[pl.ds(low, sub), at] = (o / total).astype(jnp.bfloat16)

            spot = pl.ds(low, sub)

            def project(side, c):
                at = pl.ds(pl.multiple_of(side * half + c * chunk, DH), chunk)
                return jnp.dot(ho[spot, :], w_ref[:, at], preferred_element_type=jnp.float32)

            for c in range(NC):
                sib_out[i, spot, pl.ds(c * chunk, chunk)] = project(1 - core, c).astype(
                    jnp.bfloat16
                )
                to_sibling(i, part, c).start()
            for c in range(NC):
                at = pl.ds(c * chunk, chunk)
                mine = project(core, c)
                to_sibling(i, part, c).wait_recv()
                both = mine + sib_in[i, spot, at].astype(jnp.float32)
                comb[i, spot, at] = both.astype(jnp.bfloat16)

                @pl.when(me == i)
                def _():
                    keep(i, part, c).start()

                @pl.when(me != i)
                def _():
                    to_owner(i, part, c, me, i).start()

        return carry

    lax.fori_loop(0, nh, block, 0)

    pieces = [(part, c) for part in reversed(range(NS)) for c in range(NC)]
    for part, c in pieces:
        keep(me, part, c).wait()
        for jx, jc in arrival:
            source = partner(jx, jc)
            to_owner(source, part, c, source, source).wait_recv()

    for jx, jc in arrival:
        peer = partner(jx, jc)
        swap(1, v_hbm, vbuf, 2 * seg, peer, me).wait_send()
        swap(0, kn, kbuf, 2 * seg, peer, me).wait_send()
        swap(2, qn, qseg, 0, peer, me).wait_send()
        for part, c in pieces:
            to_owner(peer, part, c, me, peer).wait_send()

    def sent(i, carry):
        for kind, buf in ((0, kbuf), (1, vbuf)):
            hop(piece(buf, 2 * seg, i), buf, kind, seg, i, h1_s, h1_r).wait_send()
            for part in range(NS):
                pass_on(kind, buf, i, part).wait_send()
        for part, c in pieces:
            to_sibling(i, part, c).wait_send()
        return carry

    lax.fori_loop(0, nh, sent, 0)


def solution(mesh):
    nh = mesh.shape["head"]
    nb = mesh.shape["blk"]

    def shards(queries, keys, values, scale_qk, w_out, stretch_start):
        t, hd = queries.shape
        cols = hd // nh
        seg = nh * t
        width = w_out.shape[1]
        half = width // 2
        bf16 = jnp.bfloat16
        dma = pltpu.SemaphoreType.DMA
        anywhere = pl.BlockSpec(memory_space=pl.ANY)
        vmem = pl.BlockSpec(memory_space=pltpu.VMEM)
        parts = pl.pallas_call(
            functools.partial(kernel, nh, nb),
            out_shape=jax.ShapeDtypeStruct((nh // 2, t, width), bf16),
            in_specs=[anywhere, anywhere, anywhere, vmem, anywhere,
                      pl.BlockSpec(memory_space=pltpu.SMEM)],
            out_specs=anywhere,
            scratch_shapes=[
                pltpu.VMEM((t, hd), bf16),
                pltpu.VMEM((t, hd), bf16),
                pltpu.VMEM((t, hd), bf16),
                pltpu.VMEM((t, hd), bf16),
                pltpu.VMEM((cols, width), bf16),
                pltpu.VMEM((seg, cols), bf16),
                pltpu.VMEM((3 * seg, cols), bf16),
                pltpu.VMEM((3 * seg, cols), bf16),
                pltpu.VMEM((t, cols), jnp.float32),
                pltpu.VMEM((t, cols), bf16),
                pltpu.VMEM((nh, t, half), bf16),
                pltpu.VMEM((nh, t, half), bf16),
                pltpu.VMEM((nh, t, half), bf16),
                dma((3,)),
                dma((3,)),
                dma((NS, NC)),
                dma((3, nh)),
                dma((3, nh)),
                dma((2, nh)),
                dma((2, nh)),
                dma((2, nh, NS)),
                dma((2, nh, NS)),
                dma((nh, NS, NC)),
                dma((nh, NS, NC)),
                dma((nh, NS, NC)),
                dma((nh, NS, NC)),
            ],
            compiler_params=pltpu.CompilerParams(
                collective_id=0, has_side_effects=True, vmem_limit_bytes=56 * 1024 * 1024
            ),
        )(queries, keys, values, scale_qk.reshape(1, hd), w_out, stretch_start)
        return jnp.sum(parts.astype(jnp.float32), axis=0).astype(bf16)

    return jax.shard_map(
        shards,
        mesh=mesh,
        in_specs=(
            P(("groups", "blk", "head"), None),
            P(("groups", "blk", "head"), None),
            P(("groups", "blk", "head"), None),
            P(),
            P("head", None),
            P(("groups", "blk", "head")),
        ),
        out_specs=P(("groups", "blk", "head"), None),
        check_vma=False,
    )
```

```python
import functools

import jax
import jax.numpy as jnp
from jax import lax
from jax.experimental import pallas as pl
from jax.experimental.pallas import tpu as pltpu
from jax.sharding import PartitionSpec as P

DH = 128
SCORE = 1.4426950408889634 / DH**0.5
NC = 2
SLOTS = 3


def kernel(
    nh, nb, q_hbm, k_hbm, v_hbm, scale_ref, w_hbm, start_ref, rbuf,
    qin, kin, qn, kn, w_ref, qseg, kbuf, vbuf, acc, ho, sib_out, sib_in, comb,
    load_sem, loc_sem, keep_sem, a2a_s, a2a_r, h1_s, h1_r, h2_s, h2_r, sib_s, sib_r, red_s, red_r,
):
    t, hd = qin.shape
    cols = hd // nh
    heads = cols // DH
    seg = nh * t
    usual = ((0, t // 2, t // 2), (1, 0, t // 2))
    final = ((0, t // 2, t // 2), (1, t // 4, t // 4), (2, 0, t // 4))
    width = w_ref.shape[1]
    half = width // 2
    chunk = half // NC
    nx = nh // 2
    me = lax.axis_index("head")
    z = lax.axis_index("blk")
    chip = me // 2
    core = me % 2
    sib = chip * 2 + (1 - core)
    nxt = (z + 1) % nb
    prv = (z + nb - 1) % nb

    def partner(jx, jc):
        return ((chip + jx) % nx) * 2 + (core + jc) % 2

    others = [(jx, 0) for jx in range(1, nx)] + [(jx, 1) for jx in range(nx)]
    arrival = [(jx, jc) for jx in range(nx) for jc in range(2) if jx or jc]

    loads = [
        pltpu.make_async_copy(k_hbm, kin, load_sem.at[0]),
        pltpu.make_async_copy(q_hbm, qin, load_sem.at[1]),
        pltpu.make_async_copy(w_hbm, w_ref, load_sem.at[2]),
    ]
    for copy in loads:
        copy.start()

    barrier = pltpu.get_barrier_semaphore()
    for jx, jc in others:
        pl.semaphore_signal(barrier, inc=1, device_id={"head": partner(jx, jc)})
    pl.semaphore_signal(barrier, inc=1, device_id={"blk": nxt})
    pl.semaphore_signal(barrier, inc=1, device_id={"blk": prv})
    pl.semaphore_wait(barrier, nh + 1)

    def group(ref, peer):
        return ref.at[:, pl.ds(pl.multiple_of(peer * cols, DH), cols)]

    def piece(ref, base, index):
        return ref.at[pl.ds(pl.multiple_of(base + index * t, t), t), :]

    def swap(kind, src, dst, base, peer, source):
        return pltpu.make_async_remote_copy(
            src_ref=group(src, peer), dst_ref=piece(dst, base, source),
            send_sem=a2a_s.at[kind, peer], recv_sem=a2a_r.at[kind, source],
            device_id={"head": peer},
        )

    def hop(src, dst, kind, base, index, send, recv):
        return pltpu.make_async_remote_copy(
            src_ref=src, dst_ref=piece(dst, base, index),
            send_sem=send.at[kind, index], recv_sem=recv.at[kind, index],
            device_id={"blk": nxt},
        )

    def normed(src, dst, peer):
        for h in range(heads):
            at = pl.ds(pl.multiple_of(peer * cols + h * DH, DH), DH)
            x = src[:, at].astype(jnp.float32)
            x = x * lax.rsqrt(jnp.mean(x * x, axis=1, keepdims=True) + 1e-06)
            dst[:, at] = (x * scale_ref[:, at]).astype(jnp.bfloat16)

    hop(group(v_hbm, me), vbuf, 1, seg, me, h1_s, h1_r).start()
    for jx, jc in others:
        swap(1, v_hbm, vbuf, 2 * seg, partner(jx, jc), me).start()
    own_v = pltpu.make_async_copy(group(v_hbm, me), piece(vbuf, 2 * seg, me), loc_sem.at[1])
    own_v.start()

    loads[0].wait()
    normed(kin, kn, me)
    hop(group(kn, me), kbuf, 0, seg, me, h1_s, h1_r).start()
    own_k = pltpu.make_async_copy(group(kn, me), piece(kbuf, 2 * seg, me), loc_sem.at[0])
    own_k.start()
    for jx, jc in others:
        peer = partner(jx, jc)
        normed(kin, kn, peer)
        swap(0, kn, kbuf, 2 * seg, peer, me).start()

    loads[1].wait()
    for jx, jc in [(0, 0)] + others:
        normed(qin, qn, partner(jx, jc))
    own_q = pltpu.make_async_copy(group(qn, me), piece(qseg, 0, me), loc_sem.at[2])
    own_q.start()

    def onward(kind, src, buf, jx, jc):
        source = partner(jx, jc)
        swap(kind, src, buf, 2 * seg, source, source).wait_recv()
        hop(piece(buf, 2 * seg, source), buf, kind, seg, source, h1_s, h1_r).start()

    onward(1, v_hbm, vbuf, 0, 1)
    onward(0, kn, kbuf, 0, 1)
    for jx, jc in arrival[1:]:
        onward(1, v_hbm, vbuf, jx, jc)
    for jx, jc in arrival[1:]:
        onward(0, kn, kbuf, jx, jc)
    for jx, jc in others:
        peer = partner(jx, jc)
        swap(2, qn, qseg, 0, peer, me).start()

    def slab(ref, base, i, low, size):
        return ref.at[pl.ds(pl.multiple_of(base + i * t + low, size), size), :]

    def pass_on(kind, buf, i, part):
        slot, low, size = part
        return pltpu.make_async_remote_copy(
            src_ref=slab(buf, seg, i, low, size), dst_ref=slab(buf, 0, i, low, size),
            send_sem=h2_s.at[kind, i, slot], recv_sem=h2_r.at[kind, i, slot],
            device_id={"blk": nxt},
        )

    def landed(kind, buf, i):
        hop(piece(buf, 2 * seg, i), buf, kind, seg, i, h1_s, h1_r).wait_recv()

    def early(i, parts):
        landed(1, vbuf, i)
        for part in parts:
            pass_on(1, vbuf, i, part).start()

    def relay(i, parts):
        landed(0, kbuf, i)

        @pl.when(i // 2 != chip)
        def _():
            landed(1, vbuf, i)
            for part in parts:
                pass_on(0, kbuf, i, part).start()
                pass_on(1, vbuf, i, part).start()

        @pl.when(i // 2 == chip)
        def _():
            for part in parts:
                pass_on(0, kbuf, i, part).start()

    for i in (me, sib):
        pl.when(i == 0)(functools.partial(early, i, final))
        pl.when(i != 0)(functools.partial(early, i, usual))

    def relay_usual(step, carry):
        relay(nh - 1 - step, usual)
        return carry

    lax.fori_loop(0, nh - 1, relay_usual, 0)
    relay(0, final)
    for jx, jc in arrival:
        source = partner(jx, jc)
        swap(2, qn, qseg, 0, source, source).wait_recv()
    own_q.wait()
    own_k.wait()
    own_v.wait()
    loads[2].wait()

    first = start_ref[0] - me * t
    row = lax.broadcasted_iota(jnp.int32, (t, 2 * seg), 0)
    col = lax.broadcasted_iota(jnp.int32, (t, 2 * seg), 1)

    def to_sibling(i, part, c):
        slot, low, size = part
        at = (i, pl.ds(low, size), pl.ds(c * chunk, chunk))
        return pltpu.make_async_remote_copy(
            src_ref=sib_out.at[at], dst_ref=sib_in.at[at],
            send_sem=sib_s.at[i, slot, c], recv_sem=sib_r.at[i, slot, c],
            device_id={"head": sib},
        )

    def home(x, side, part, c):
        slot, low, size = part
        columns = pl.ds(pl.multiple_of(side * half + c * chunk, DH), chunk)
        return rbuf.at[x, pl.ds(low, size), columns]

    def to_owner(i, part, c, source, owner):
        slot, low, size = part
        return pltpu.make_async_remote_copy(
            src_ref=comb.at[i, pl.ds(low, size), pl.ds(c * chunk, chunk)],
            dst_ref=home(source // 2, source % 2, part, c),
            send_sem=red_s.at[i, slot, c], recv_sem=red_r.at[source, slot, c],
            device_id={"head": owner},
        )

    def keep(i, part, c):
        slot, low, size = part
        return pltpu.make_async_copy(
            comb.at[i, pl.ds(low, size), pl.ds(c * chunk, chunk)],
            home(chip, core, part, c), keep_sem.at[slot, c],
        )

    def block(i, parts):
        rows = pl.ds(pl.multiple_of(i * t, t), t)
        keys = pl.ds(pl.multiple_of(i * t + t, t), 2 * seg)
        oldest = 2 * seg - first - i * t
        allowed = (col <= row + (2 * seg - t)) & (col >= oldest - t)
        held = []
        for h in range(heads):
            at = pl.ds(h * DH, DH)
            s = lax.dot_general(
                qseg[rows, at], kbuf[keys, at], (((1,), (1,)), ((), ())),
                preferred_element_type=jnp.float32,
            )
            s = jnp.where(allowed, s, -1e30)
            peak = jnp.max(s, axis=1, keepdims=True)
            p = jnp.exp2((s - peak) * SCORE)
            held.append((peak, jnp.sum(p, axis=1, keepdims=True)))
            acc[:, at] = jnp.dot(
                p.astype(jnp.bfloat16), vbuf[keys, at], preferred_element_type=jnp.float32
            )

        for part in parts:
            for kind, buf in ((0, kbuf), (1, vbuf)):
                pass_on(kind, buf, i, part).wait_recv()
            slot, low, sub = part
            many = t - low
            keys = pl.ds(pl.multiple_of(i * t + low, sub), many)
            here = pl.ds(pl.multiple_of(i * t + low, sub), sub)
            age = lax.broadcasted_iota(jnp.int32, (sub, many), 1)
            allowed = (age > lax.broadcasted_iota(jnp.int32, (sub, many), 0)) & (
                age >= oldest - low
            )
            for h in range(heads):
                at = pl.ds(h * DH, DH)
                s = lax.dot_general(
                    qseg[here, at], kbuf[keys, at], (((1,), (1,)), ((), ())),
                    preferred_element_type=jnp.float32,
                )
                s = jnp.where(allowed, s, -1e30)
                peak, total = (value[low:low + sub] for value in held[h])
                top = jnp.maximum(peak, jnp.max(s, axis=1, keepdims=True))
                p = jnp.exp2((s - top) * SCORE)
                fade = jnp.exp2((peak - top) * SCORE)
                total = total * fade + jnp.sum(p, axis=1, keepdims=True)
                o = acc[pl.ds(low, sub), at] * fade + jnp.dot(
                    p.astype(jnp.bfloat16), vbuf[keys, at], preferred_element_type=jnp.float32
                )
                ho[pl.ds(low, sub), at] = (o / total).astype(jnp.bfloat16)

            spot = pl.ds(low, sub)

            def project(side, c):
                at = pl.ds(pl.multiple_of(side * half + c * chunk, DH), chunk)
                return jnp.dot(ho[spot, :], w_ref[:, at], preferred_element_type=jnp.float32)

            for c in range(NC):
                at = pl.ds(c * chunk, chunk)
                sib_out[i, spot, at] = project(1 - core, c).astype(jnp.bfloat16)
                to_sibling(i, part, c).start()
                mine = project(core, c)
                to_sibling(i, part, c).wait_recv()
                both = mine + sib_in[i, spot, at].astype(jnp.float32)
                comb[i, spot, at] = both.astype(jnp.bfloat16)

                @pl.when(me == i)
                def _():
                    keep(i, part, c).start()

                @pl.when(me != i)
                def _():
                    to_owner(i, part, c, me, i).start()

    def block_usual(step, carry):
        block(nh - 1 - step, usual)
        return carry

    lax.fori_loop(0, nh - 1, block_usual, 0)
    block(0, final)

    def collect(parts):
        for part in parts:
            for c in range(NC):
                keep(me, part, c).wait()
                for jx, jc in arrival:
                    source = partner(jx, jc)
                    to_owner(source, part, c, source, source).wait_recv()

    @pl.when(me == 0)
    def _():
        collect(final)

    @pl.when(me != 0)
    def _():
        collect(usual)

    for jx, jc in arrival:
        peer = partner(jx, jc)
        swap(1, v_hbm, vbuf, 2 * seg, peer, me).wait_send()
        swap(0, kn, kbuf, 2 * seg, peer, me).wait_send()
        swap(2, qn, qseg, 0, peer, me).wait_send()

    def sent(i, parts):
        for kind, buf in ((0, kbuf), (1, vbuf)):
            hop(piece(buf, 2 * seg, i), buf, kind, seg, i, h1_s, h1_r).wait_send()
            for part in parts:
                pass_on(kind, buf, i, part).wait_send()
        for part in parts:
            for c in range(NC):
                to_sibling(i, part, c).wait_send()

        @pl.when(me != i)
        def _():
            for part in parts:
                for c in range(NC):
                    to_owner(i, part, c, me, i).wait_send()

    def sent_usual(step, carry):
        sent(step + 1, usual)
        return carry

    lax.fori_loop(0, nh - 1, sent_usual, 0)
    sent(0, final)


def solution(mesh):
    nh = mesh.shape["head"]
    nb = mesh.shape["blk"]

    def shards(queries, keys, values, scale_qk, w_out, stretch_start):
        t, hd = queries.shape
        cols = hd // nh
        seg = nh * t
        width = w_out.shape[1]
        half = width // 2
        bf16 = jnp.bfloat16
        dma = pltpu.SemaphoreType.DMA
        anywhere = pl.BlockSpec(memory_space=pltpu.HBM)
        vmem = pl.BlockSpec(memory_space=pltpu.VMEM)
        parts = pl.pallas_call(
            functools.partial(kernel, nh, nb),
            out_shape=pltpu.VMEM((nh // 2, t, width), bf16),
            in_specs=[anywhere, anywhere, anywhere, vmem, anywhere,
                      pl.BlockSpec(memory_space=pltpu.SMEM)],
            out_specs=vmem,
            scratch_shapes=[
                pltpu.VMEM((t, hd), bf16),
                pltpu.VMEM((t, hd), bf16),
                pltpu.VMEM((t, hd), bf16),
                pltpu.VMEM((t, hd), bf16),
                pltpu.VMEM((cols, width), bf16),
                pltpu.VMEM((seg, cols), bf16),
                pltpu.VMEM((3 * seg, cols), bf16),
                pltpu.VMEM((3 * seg, cols), bf16),
                pltpu.VMEM((t, cols), jnp.float32),
                pltpu.VMEM((t, cols), bf16),
                pltpu.VMEM((nh, t, half), bf16),
                pltpu.VMEM((nh, t, half), bf16),
                pltpu.VMEM((nh, t, half), bf16),
                dma((3,)),
                dma((3,)),
                dma((SLOTS, NC)),
                dma((3, nh)),
                dma((3, nh)),
                dma((2, nh)),
                dma((2, nh)),
                dma((2, nh, SLOTS)),
                dma((2, nh, SLOTS)),
                dma((nh, SLOTS, NC)),
                dma((nh, SLOTS, NC)),
                dma((nh, SLOTS, NC)),
                dma((nh, SLOTS, NC)),
            ],
            compiler_params=pltpu.CompilerParams(
                collective_id=0, has_side_effects=True, vmem_limit_bytes=54 * 1024 * 1024
            ),
        )(queries, keys, values, scale_qk.reshape(1, hd), w_out, stretch_start)
        return jnp.sum(parts.astype(jnp.float32), axis=0).astype(bf16)

    return jax.shard_map(
        shards,
        mesh=mesh,
        in_specs=(
            P(("groups", "blk", "head"), None),
            P(("groups", "blk", "head"), None),
            P(("groups", "blk", "head"), None),
            P(),
            P("head", None),
            P(("groups", "blk", "head")),
        ),
        out_specs=P(("groups", "blk", "head"), None),
        check_vma=False,
    )
```

```python
import functools

import jax
import jax.numpy as jnp
from jax import lax
from jax.experimental import pallas as pl
from jax.experimental.pallas import tpu as pltpu
from jax.sharding import PartitionSpec as P

DH = 128
SCORE = 1.4426950408889634 / DH**0.5
NC = 2
NS = 2


def kernel(
    nh, nb, q_hbm, k_hbm, v_hbm, scale_ref, w_hbm, start_ref, rbuf,
    qin, kin, qn, kn, w_ref, qseg, kbuf, vbuf, acc, ho, sib_out, sib_in, comb,
    load_sem, loc_sem, keep_sem, a2a_s, a2a_r, h1_s, h1_r, h2_s, h2_r, sib_s, sib_r, red_s, red_r,
):
    t, hd = qin.shape
    cols = hd // nh
    heads = cols // DH
    seg = nh * t
    sub = t // NS
    width = w_ref.shape[1]
    half = width // 2
    chunk = half // NC
    nx = nh // 2
    me = lax.axis_index("head")
    z = lax.axis_index("blk")
    chip = me // 2
    core = me % 2
    sib = chip * 2 + (1 - core)
    nxt = (z + 1) % nb
    prv = (z + nb - 1) % nb

    def partner(jx, jc):
        return ((chip + jx) % nx) * 2 + (core + jc) % 2

    others = [(jx, 0) for jx in range(1, nx)] + [(jx, 1) for jx in range(nx)]
    arrival = [(jx, jc) for jx in range(nx) for jc in range(2) if jx or jc]

    loads = [
        pltpu.make_async_copy(k_hbm, kin, load_sem.at[0]),
        pltpu.make_async_copy(q_hbm, qin, load_sem.at[1]),
        pltpu.make_async_copy(w_hbm, w_ref, load_sem.at[2]),
    ]
    for copy in loads:
        copy.start()

    barrier = pltpu.get_barrier_semaphore()
    for jx, jc in others:
        pl.semaphore_signal(barrier, inc=1, device_id={"head": partner(jx, jc)})
    pl.semaphore_signal(barrier, inc=1, device_id={"blk": nxt})
    pl.semaphore_signal(barrier, inc=1, device_id={"blk": prv})
    pl.semaphore_wait(barrier, nh + 1)

    def group(ref, peer):
        return ref.at[:, pl.ds(pl.multiple_of(peer * cols, DH), cols)]

    def piece(ref, base, index):
        return ref.at[pl.ds(pl.multiple_of(base + index * t, t), t), :]

    def swap(kind, src, dst, base, peer, source):
        return pltpu.make_async_remote_copy(
            src_ref=group(src, peer), dst_ref=piece(dst, base, source),
            send_sem=a2a_s.at[kind, peer], recv_sem=a2a_r.at[kind, source],
            device_id={"head": peer},
        )

    def hop(src, dst, kind, base, index, send, recv):
        return pltpu.make_async_remote_copy(
            src_ref=src, dst_ref=piece(dst, base, index),
            send_sem=send.at[kind, index], recv_sem=recv.at[kind, index],
            device_id={"blk": nxt},
        )

    def normed(src, dst, peer):
        for h in range(heads):
            at = pl.ds(pl.multiple_of(peer * cols + h * DH, DH), DH)
            x = src[:, at].astype(jnp.float32)
            x = x * lax.rsqrt(jnp.mean(x * x, axis=1, keepdims=True) + 1e-06)
            dst[:, at] = (x * scale_ref[:, at]).astype(jnp.bfloat16)

    hop(group(v_hbm, me), vbuf, 1, seg, me, h1_s, h1_r).start()
    for jx, jc in others:
        swap(1, v_hbm, vbuf, 2 * seg, partner(jx, jc), me).start()
    own_v = pltpu.make_async_copy(group(v_hbm, me), piece(vbuf, 2 * seg, me), loc_sem.at[1])
    own_v.start()

    loads[0].wait()
    normed(kin, kn, me)
    hop(group(kn, me), kbuf, 0, seg, me, h1_s, h1_r).start()
    own_k = pltpu.make_async_copy(group(kn, me), piece(kbuf, 2 * seg, me), loc_sem.at[0])
    own_k.start()
    for jx, jc in others:
        peer = partner(jx, jc)
        normed(kin, kn, peer)
        swap(0, kn, kbuf, 2 * seg, peer, me).start()

    loads[1].wait()
    for jx, jc in [(0, 0)] + others:
        normed(qin, qn, partner(jx, jc))
    own_q = pltpu.make_async_copy(group(qn, me), piece(qseg, 0, me), loc_sem.at[2])
    own_q.start()

    def onward(kind, src, buf, jx, jc):
        source = partner(jx, jc)
        swap(kind, src, buf, 2 * seg, source, source).wait_recv()
        hop(piece(buf, 2 * seg, source), buf, kind, seg, source, h1_s, h1_r).start()

    onward(1, v_hbm, vbuf, 0, 1)
    onward(0, kn, kbuf, 0, 1)
    for jx, jc in arrival[1:]:
        onward(1, v_hbm, vbuf, jx, jc)
    for jx, jc in arrival[1:]:
        onward(0, kn, kbuf, jx, jc)
    for jx, jc in others:
        peer = partner(jx, jc)
        swap(2, qn, qseg, 0, peer, me).start()

    def slab(ref, base, i, part):
        return ref.at[pl.ds(pl.multiple_of(base + i * t + part * sub, sub), sub), :]

    def pass_on(kind, buf, i, part):
        return pltpu.make_async_remote_copy(
            src_ref=slab(buf, seg, i, part), dst_ref=slab(buf, 0, i, part),
            send_sem=h2_s.at[kind, i, part], recv_sem=h2_r.at[kind, i, part],
            device_id={"blk": nxt},
        )

    def relay(step, carry):
        i = nh - 1 - step
        for kind, buf in ((0, kbuf), (1, vbuf)):
            hop(piece(buf, 2 * seg, i), buf, kind, seg, i, h1_s, h1_r).wait_recv()
        for part in reversed(range(NS)):
            for kind, buf in ((0, kbuf), (1, vbuf)):
                pass_on(kind, buf, i, part).start()
        return carry

    lax.fori_loop(0, nh, relay, 0)
    for jx, jc in arrival:
        source = partner(jx, jc)
        swap(2, qn, qseg, 0, source, source).wait_recv()
    own_q.wait()
    own_k.wait()
    own_v.wait()
    loads[2].wait()

    first = start_ref[0] - me * t
    row = lax.broadcasted_iota(jnp.int32, (t, 2 * seg), 0)
    col = lax.broadcasted_iota(jnp.int32, (t, 2 * seg), 1)

    def to_sibling(i, part, c):
        at = (i, pl.ds(part * sub, sub), pl.ds(c * chunk, chunk))
        return pltpu.make_async_remote_copy(
            src_ref=sib_out.at[at], dst_ref=sib_in.at[at],
            send_sem=sib_s.at[i, part, c], recv_sem=sib_r.at[i, part, c],
            device_id={"head": sib},
        )

    def home(x, side, part, c):
        columns = pl.ds(pl.multiple_of(side * half + c * chunk, DH), chunk)
        return rbuf.at[x, pl.ds(part * sub, sub), columns]

    def to_owner(i, part, c, source, owner):
        return pltpu.make_async_remote_copy(
            src_ref=comb.at[i, pl.ds(part * sub, sub), pl.ds(c * chunk, chunk)],
            dst_ref=home(source // 2, source % 2, part, c),
            send_sem=red_s.at[i, part, c], recv_sem=red_r.at[source, part, c],
            device_id={"head": owner},
        )

    def keep(i, part, c):
        return pltpu.make_async_copy(
            comb.at[i, pl.ds(part * sub, sub), pl.ds(c * chunk, chunk)],
            home(chip, core, part, c), keep_sem.at[part, c],
        )

    def block(step, carry):
        i = nh - 1 - step
        rows = pl.ds(pl.multiple_of(i * t, t), t)
        keys = pl.ds(pl.multiple_of(i * t + t, t), 2 * seg)
        oldest = 2 * seg - first - i * t
        allowed = (col <= row + (2 * seg - t)) & (col >= oldest - t)
        held = []
        for h in range(heads):
            at = pl.ds(h * DH, DH)
            s = lax.dot_general(
                qseg[rows, at], kbuf[keys, at], (((1,), (1,)), ((), ())),
                preferred_element_type=jnp.float32,
            )
            s = jnp.where(allowed, s, -1e30)
            peak = jnp.max(s, axis=1, keepdims=True)
            p = jnp.exp2((s - peak) * SCORE)
            held.append((peak, jnp.sum(p, axis=1, keepdims=True)))
            acc[:, at] = jnp.dot(
                p.astype(jnp.bfloat16), vbuf[keys, at], preferred_element_type=jnp.float32
            )

        for part in reversed(range(NS)):
            for kind, buf in ((0, kbuf), (1, vbuf)):
                pass_on(kind, buf, i, part).wait_recv()
            low = part * sub
            many = t - low
            keys = pl.ds(pl.multiple_of(i * t + low, sub), many)
            here = pl.ds(pl.multiple_of(i * t + low, sub), sub)
            age = lax.broadcasted_iota(jnp.int32, (sub, many), 1)
            allowed = (age > lax.broadcasted_iota(jnp.int32, (sub, many), 0)) & (
                age >= oldest - low
            )
            for h in range(heads):
                at = pl.ds(h * DH, DH)
                s = lax.dot_general(
                    qseg[here, at], kbuf[keys, at], (((1,), (1,)), ((), ())),
                    preferred_element_type=jnp.float32,
                )
                s = jnp.where(allowed, s, -1e30)
                peak, total = (value[low:low + sub] for value in held[h])
                top = jnp.maximum(peak, jnp.max(s, axis=1, keepdims=True))
                p = jnp.exp2((s - top) * SCORE)
                fade = jnp.exp2((peak - top) * SCORE)
                total = total * fade + jnp.sum(p, axis=1, keepdims=True)
                o = acc[pl.ds(low, sub), at] * fade + jnp.dot(
                    p.astype(jnp.bfloat16), vbuf[keys, at], preferred_element_type=jnp.float32
                )
                ho[pl.ds(low, sub), at] = (o / total).astype(jnp.bfloat16)

            spot = pl.ds(low, sub)

            def project(side, c):
                at = pl.ds(pl.multiple_of(side * half + c * chunk, DH), chunk)
                return jnp.dot(ho[spot, :], w_ref[:, at], preferred_element_type=jnp.float32)

            for c in range(NC):
                sib_out[i, spot, pl.ds(c * chunk, chunk)] = project(1 - core, c).astype(
                    jnp.bfloat16
                )
                to_sibling(i, part, c).start()
            for c in range(NC):
                at = pl.ds(c * chunk, chunk)
                mine = project(core, c)
                to_sibling(i, part, c).wait_recv()
                both = mine + sib_in[i, spot, at].astype(jnp.float32)
                comb[i, spot, at] = both.astype(jnp.bfloat16)

                @pl.when(me == i)
                def _():
                    keep(i, part, c).start()

                @pl.when(me != i)
                def _():
                    to_owner(i, part, c, me, i).start()

        return carry

    lax.fori_loop(0, nh, block, 0)

    pieces = [(part, c) for part in reversed(range(NS)) for c in range(NC)]
    for part, c in pieces:
        keep(me, part, c).wait()
        for jx, jc in arrival:
            source = partner(jx, jc)
            to_owner(source, part, c, source, source).wait_recv()

    for jx, jc in arrival:
        peer = partner(jx, jc)
        swap(1, v_hbm, vbuf, 2 * seg, peer, me).wait_send()
        swap(0, kn, kbuf, 2 * seg, peer, me).wait_send()
        swap(2, qn, qseg, 0, peer, me).wait_send()
        for part, c in pieces:
            to_owner(peer, part, c, me, peer).wait_send()

    def sent(i, carry):
        for kind, buf in ((0, kbuf), (1, vbuf)):
            hop(piece(buf, 2 * seg, i), buf, kind, seg, i, h1_s, h1_r).wait_send()
            for part in range(NS):
                pass_on(kind, buf, i, part).wait_send()
        for part, c in pieces:
            to_sibling(i, part, c).wait_send()
        return carry

    lax.fori_loop(0, nh, sent, 0)


def solution(mesh):
    nh = mesh.shape["head"]
    nb = mesh.shape["blk"]

    def shards(queries, keys, values, scale_qk, w_out, stretch_start):
        t, hd = queries.shape
        cols = hd // nh
        seg = nh * t
        width = w_out.shape[1]
        half = width // 2
        bf16 = jnp.bfloat16
        dma = pltpu.SemaphoreType.DMA
        anywhere = pl.BlockSpec(memory_space=pltpu.HBM)
        vmem = pl.BlockSpec(memory_space=pltpu.VMEM)
        parts = pl.pallas_call(
            functools.partial(kernel, nh, nb),
            out_shape=pltpu.VMEM((nh // 2, t, width), bf16),
            in_specs=[anywhere, anywhere, anywhere, vmem, anywhere,
                      pl.BlockSpec(memory_space=pltpu.SMEM)],
            out_specs=vmem,
            scratch_shapes=[
                pltpu.VMEM((t, hd), bf16),
                pltpu.VMEM((t, hd), bf16),
                pltpu.VMEM((t, hd), bf16),
                pltpu.VMEM((t, hd), bf16),
                pltpu.VMEM((cols, width), bf16),
                pltpu.VMEM((seg, cols), bf16),
                pltpu.VMEM((3 * seg, cols), bf16),
                pltpu.VMEM((3 * seg, cols), bf16),
                pltpu.VMEM((t, cols), jnp.float32),
                pltpu.VMEM((t, cols), bf16),
                pltpu.VMEM((nh, t, half), bf16),
                pltpu.VMEM((nh, t, half), bf16),
                pltpu.VMEM((nh, t, half), bf16),
                dma((3,)),
                dma((3,)),
                dma((NS, NC)),
                dma((3, nh)),
                dma((3, nh)),
                dma((2, nh)),
                dma((2, nh)),
                dma((2, nh, NS)),
                dma((2, nh, NS)),
                dma((nh, NS, NC)),
                dma((nh, NS, NC)),
                dma((nh, NS, NC)),
                dma((nh, NS, NC)),
            ],
            compiler_params=pltpu.CompilerParams(
                collective_id=0, has_side_effects=True, vmem_limit_bytes=54 * 1024 * 1024
            ),
        )(queries, keys, values, scale_qk.reshape(1, hd), w_out, stretch_start)
        return jnp.sum(parts.astype(jnp.float32), axis=0).astype(bf16)

    return jax.shard_map(
        shards,
        mesh=mesh,
        in_specs=(
            P(("groups", "blk", "head"), None),
            P(("groups", "blk", "head"), None),
            P(("groups", "blk", "head"), None),
            P(),
            P("head", None),
            P(("groups", "blk", "head")),
        ),
        out_specs=P(("groups", "blk", "head"), None),
        check_vma=False,
    )
```
